256 devices in a mesh: section: 4 (over x), expert: 64 (over z, y, core).
Axes of the slice: x: 4, y: 4, z: 8, core: 2. Of those that a mesh axis runs over, the one named last changes fastest.
Arguments:
- inputs: bfloat16 [2, 4096, 2048], P(None, 'expert'), may hold values from -45 to 45
- cotangent: bfloat16 [2, 4096, 2048], P(None, 'expert'), may hold values from -6 to 6
- lengths: int32 [2, 64], P(None, 'expert'), may hold values from 32 to 64, as said below
- norm_gain: float32 [4, 2048], P('section'), may hold values from 0.1 to 1.9
- router: bfloat16 [4, 2048, 64], P('section'), may hold values from -0.125 to 0.125
- expert_in: bfloat16 [4, 64, 2048, 1536], P('section', 'expert'), may hold values from -0.125 to 0.125
- expert_out: bfloat16 [4, 64, 768, 2048], P('section', 'expert'), may hold values from -0.21875 to 0.21875
- routes: int32 [4, 2, 4096, 2], P('section', None, 'expert'), may hold values from 0 to 63, as said below
Outputs:
- section_grads: bfloat16 [4, 2, 4096, 2048], P('section', None, 'expert')
- router_grad: float32 [4, 2048, 64], P('section')
- gain_grad: float32 [4, 2048], P('section')
The draws below stay inside these ranges and needn't reach their ends.
Inputs may be any that keep to these rules, and one draw needn't show every extreme that they name: `lengths`: sequence b of a micro-batch fills positions b * 64 to b * 64 + length - 1; the rest is padding. Each micro-batch has a sequence of length 64. `routes`: each row names 2 different experts. Among the rows of one sequence for one section and micro-batch no expert is named more than 2 times; for each section and micro-batch one expert is named exactly 2 times within the first 32 rows of every sequence. For each section and micro-batch the experts fall into two halves, a row's first choice in one and its second in the other.
All inputs are finite; a program needn't handle non-finite values.
Results may differ from the reference program's by a relative error of at most 0.024.
Values may be sent and summed in bfloat16 or wider, within the bound.
A program may use at most 128 MiB of HBM per device.

```python
import math
import jax
import jax.numpy as jnp
from jax import lax

D = 2048
F = 768
TOPK = 2
MICRO = 2
TOK_DEV = 64
EXPERTS = 64
SECTIONS = 4
SEQS = 64
TOKENS = 4096
CAP = 2
N_EXPERT = 64


def draw_inputs(key, part):
    key_rows, key_cols, key_vals = jax.random.split(key, 3)
    row_scale = jnp.exp(jax.random.uniform(key_rows, (MICRO, TOKENS, 1), jnp.float32, math.log(0.3), math.log(3.0)))
    col_scale = jnp.exp(jax.random.uniform(key_cols, (1, 1, D), jnp.float32, math.log(0.3), math.log(3.0)))
    base_values = jnp.clip(jax.random.normal(key_vals, (MICRO, TOKENS, D), jnp.float32), -5.0, 5.0)
    return (base_values * row_scale * col_scale).astype(jnp.bfloat16)


def draw_lengths(key, part):
    key_len, key_full = jax.random.split(key)
    drawn_lengths = jax.random.randint(key_len, (MICRO, SEQS), TOK_DEV // 2, TOK_DEV + 1)
    full_at = jax.random.randint(key_full, (MICRO, 1), 0, SEQS)
    sequence_ids = jnp.arange(SEQS, dtype=jnp.int32)[None, :]
    return jnp.where(sequence_ids == full_at, TOK_DEV, drawn_lengths).astype(jnp.int32)


def route_block(block_key, group_first, group_second):
    key_hot, key_rest, key_second = jax.random.split(block_key, 3)
    rest_count = (EXPERTS // 2 - 1) * CAP
    hot_rows = jax.random.permutation(key_hot, TOK_DEV // 2)[:CAP]
    hot_mask = jnp.zeros((TOK_DEV,), jnp.int32).at[hot_rows].set(1)
    rest_order = jax.random.permutation(key_rest, rest_count)
    rest_rank = jnp.clip(jnp.cumsum(1 - hot_mask) - 1, 0, rest_count - 1)
    first_pick = jnp.where(hot_mask > 0, group_first[0], group_first[1 + rest_order[rest_rank] // CAP])
    second_order = jax.random.permutation(key_second, EXPERTS // 2 * CAP)
    second_pick = group_second[second_order[:TOK_DEV] // CAP]
    return jnp.stack([first_pick, second_pick], axis=1)


def draw_routes(key, part):
    group_keys = jax.random.split(jax.random.fold_in(key, 11), SECTIONS * MICRO)

    def draw_group(group_key):
        key_perm, key_blocks = jax.random.split(group_key)
        expert_order = jax.random.permutation(key_perm, EXPERTS)
        group_first = expert_order[:EXPERTS // 2]
        group_second = expert_order[EXPERTS // 2:]
        block_keys = jax.random.split(key_blocks, SEQS)

        def one_block(block_key):
            return route_block(block_key, group_first, group_second)
        return jax.vmap(one_block)(block_keys).reshape(TOKENS, 2)
    return jax.vmap(draw_group)(group_keys).reshape(SECTIONS, MICRO, TOKENS, 2).astype(jnp.int32)


def level_of(key, extent, cuts, smallest, top_value):
    level, own = 1.0, jax.random.fold_in(key, 6)
    for dim, shards_of in cuts:
        steps = jnp.exp(jax.random.uniform(jax.random.fold_in(own, dim), (shards_of,), jnp.float32, smallest / len(cuts), top_value / len(cuts)))
        level = level * jnp.repeat(steps, extent[dim] // shards_of).reshape([-1 if axis == dim else 1 for axis in range(len(extent))])
    return level


def noise(rng, shape, scale, most, cuts=(), kind=jnp.bfloat16):
    entries = jax.random.normal(rng, shape, jnp.float32) * scale
    if len(cuts) > 0:
        entries = level_of(rng, shape, cuts, -0.22, 0.18) * entries
    return jnp.clip(entries, min=-most, max=most).astype(kind)


def setup_inputs(seed: int = 0) -> dict:
    streams_of = jax.random.split(jax.random.key(seed), 9)
    inputs = draw_inputs(jax.random.fold_in(streams_of[8], 71), 0)
    cotangent = noise(streams_of[1], (MICRO, TOKENS, D), 1.0, 6.0, ((1, 64),))
    lengths = draw_lengths(jax.random.fold_in(streams_of[8], 71), 0)
    norm_gain = jnp.clip(1.0 + 0.18 * jax.random.normal(streams_of[3], (SECTIONS, D), jnp.float32), 0.1, 1.9)
    router = noise(streams_of[4], (SECTIONS, D, EXPERTS), D ** -0.5, 0.125, ((0, 4),))
    expert_in = noise(streams_of[5], (SECTIONS, EXPERTS, D, 2 * F), D ** -0.5, 0.125, ((0, 4), (1, 64)))
    expert_out = noise(streams_of[6], (SECTIONS, EXPERTS, F, D), F ** -0.5, 0.21875, ((0, 4), (1, 64)))
    routes = draw_routes(jax.random.fold_in(streams_of[8], 71), 0)
    return {"inputs": inputs, "cotangent": cotangent, "lengths": lengths, "norm_gain": norm_gain, "router": router, "expert_in": expert_in, "expert_out": expert_out, "routes": routes}


EPSILON = 1e-06

def normalize(hidden_in, gain_row):
    values = hidden_in.astype(jnp.float32)
    scale_inv = lax.rsqrt(lax.optimization_barrier(jnp.mean(values * values, axis=-1, keepdims=True)) + EPSILON)
    normed = (values * scale_inv * gain_row).astype(jnp.bfloat16)
    return (values, scale_inv, normed)

def expert_mix(row_block, weight_in):
    return jnp.dot(row_block, weight_in, preferred_element_type=jnp.float32)

def expert_apply(row_block, weight_in, weight_out):
    hidden = weight_out.shape[0]
    mixed_rows = expert_mix(row_block, weight_in)
    gate_part = mixed_rows[:, :hidden]
    up_part = mixed_rows[:, hidden:]
    activated = (gate_part * jax.nn.sigmoid(gate_part) * up_part).astype(jnp.bfloat16)
    return jnp.dot(activated, weight_out, preferred_element_type=jnp.float32).astype(jnp.bfloat16)

def expert_adjoint(mixed_rows, grad_rows, weight_in, weight_out):
    hidden = weight_out.shape[0]
    gate_part = mixed_rows[:, :hidden]
    up_part = mixed_rows[:, hidden:]
    act_grad = jnp.dot(grad_rows, weight_out.T, preferred_element_type=jnp.float32)
    sigmoid_gate = jax.nn.sigmoid(gate_part)
    gate_grad = act_grad * up_part * sigmoid_gate * (1.0 + gate_part * (1.0 - sigmoid_gate))
    up_grad = act_grad * gate_part * sigmoid_gate
    joined = jnp.concatenate([gate_grad, up_grad], axis=1).astype(jnp.bfloat16)
    return jnp.dot(joined, weight_in.T, preferred_element_type=jnp.float32).astype(jnp.bfloat16)

def route_weights(normed, router_section, route_rows):
    logits = jnp.dot(normed, router_section, preferred_element_type=jnp.float32)
    picked = jnp.take_along_axis(logits, route_rows, axis=1)
    return jax.nn.sigmoid(picked - picked[:, ::-1])

def expert_rows_of(pair_experts, pair_live, expert_id, most_rows):
    selected = (pair_experts == expert_id) & pair_live
    indices = jnp.nonzero(selected, size=most_rows, fill_value=0)[0].astype(jnp.int32)
    valid_rows = jnp.arange(most_rows) < jnp.sum(selected.astype(jnp.int32))
    return (indices, valid_rows)

def reference(inputs, cotangent, lengths, norm_gain, router, expert_in, expert_out, routes):
    most_rows = N_EXPERT * CAP
    pair_count = TOKENS * TOPK
    seq_of = jnp.arange(TOKENS) // TOK_DEV
    pos_in = jnp.arange(TOKENS) % TOK_DEV
    live_all = pos_in[None, :] < lengths[:, seq_of]
    expert_ids = jnp.arange(EXPERTS, dtype=jnp.int32)
    current = [inputs[micro_pos] for micro_pos in range(MICRO)]
    saved_inputs = []
    saved_pairs = []
    for section_pos in range(SECTIONS):
        gain_row = norm_gain[section_pos]
        router_section = router[section_pos]
        weight_in_all = expert_in[section_pos]
        weight_out_all = expert_out[section_pos]
        section_in = []
        section_pairs = []
        for micro_pos in range(MICRO):
            hidden_in = current[micro_pos]
            route_rows = routes[section_pos, micro_pos]
            pair_experts = route_rows.reshape(-1)
            pair_live = jnp.repeat(live_all[micro_pos], TOPK)

            def forward_layer(hidden_arg):
                values, scale_inv, normed = normalize(hidden_arg, gain_row)
                weights = route_weights(normed, router_section, route_rows)

                def one_expert(packed):
                    weight_in, weight_out, expert_id = packed
                    indices, valid_rows = expert_rows_of(pair_experts, pair_live, expert_id, most_rows)
                    result = expert_apply(normed[indices // TOPK], weight_in, weight_out)
                    return (indices, jnp.where(valid_rows[:, None], result, jnp.zeros_like(result)))
                indices, results = lax.map(one_expert, (weight_in_all, weight_out_all, expert_ids))
                pair_rows = jnp.zeros((pair_count, D), jnp.bfloat16).at[indices.reshape(-1)].add(results.reshape(-1, D))
                per_choice = pair_rows.reshape(TOKENS, TOPK, D).astype(jnp.float32)
                combined = lax.optimization_barrier(jnp.sum(weights[:, :, None] * per_choice, axis=1))
                return ((values + combined).astype(jnp.bfloat16), pair_rows)
            updated, pair_rows = forward_layer(hidden_in)
            section_in.append(hidden_in)
            section_pairs.append(pair_rows)
            current[micro_pos] = updated
        saved_inputs.append(section_in)
        saved_pairs.append(section_pairs)
    denominator = MICRO * TOPK * TOK_DEV
    grads_next = [cotangent[micro_pos] for micro_pos in range(MICRO)]
    section_list = [None] * SECTIONS
    router_list = [None] * SECTIONS
    gain_list = [None] * SECTIONS
    for section_pos in reversed(range(SECTIONS)):
        gain_row = norm_gain[section_pos]
        router_section = router[section_pos]
        weight_in_all = expert_in[section_pos]
        weight_out_all = expert_out[section_pos]
        router_sum = jnp.zeros((D, EXPERTS), jnp.float32)
        gain_sum = jnp.zeros((D,), jnp.float32)
        section_rows = []
        for micro_pos in range(MICRO):
            route_rows = routes[section_pos, micro_pos]
            pair_experts = route_rows.reshape(-1)
            pair_live = jnp.repeat(live_all[micro_pos], TOPK)

            def backward_layer(packed):
                hidden_arg, pair_rows, grad_arg = packed
                grad_values = grad_arg.astype(jnp.float32)
                values, scale_inv, normed = normalize(hidden_arg, gain_row)
                weights = route_weights(normed, router_section, route_rows)
                per_choice = pair_rows.reshape(TOKENS, TOPK, D).astype(jnp.float32)
                choice_grad = lax.optimization_barrier(jnp.sum(grad_values[:, None, :] * per_choice, axis=-1))
                first_grad = weights[:, 0] * weights[:, 1] * (choice_grad[:, 0] - choice_grad[:, 1])
                pick_grad = jnp.stack([first_grad, -first_grad], axis=1)
                chosen = route_rows[:, :, None] == expert_ids[None, None, :]
                logit_grad = lax.optimization_barrier(jnp.sum(jnp.where(chosen, pick_grad[:, :, None], 0.0), axis=1)).astype(jnp.bfloat16)
                output_grad = (weights[:, :, None] * grad_values[:, None, :]).astype(jnp.bfloat16).reshape(pair_count, D)

                def one_expert(packed_expert):
                    weight_in, weight_out, expert_id = packed_expert
                    indices, valid_rows = expert_rows_of(pair_experts, pair_live, expert_id, most_rows)
                    mixed_rows = expert_mix(normed[indices // TOPK], weight_in)
                    result = expert_adjoint(mixed_rows, output_grad[indices], weight_in, weight_out)
                    return (indices, jnp.where(valid_rows[:, None], result, jnp.zeros_like(result)))
                indices, results = lax.map(one_expert, (weight_in_all, weight_out_all, expert_ids))
                back_rows = jnp.zeros((pair_count, D), jnp.bfloat16).at[indices.reshape(-1)].add(results.reshape(-1, D))
                normed_grad = lax.optimization_barrier(jnp.sum(back_rows.reshape(TOKENS, TOPK, D).astype(jnp.float32), axis=1))
                normed_grad = normed_grad + jnp.dot(logit_grad, router_section.T, preferred_element_type=jnp.float32)
                centred = values * scale_inv
                scaled_grad = normed_grad * gain_row
                input_grad = grad_values + scale_inv * (scaled_grad - centred * lax.optimization_barrier(jnp.mean(scaled_grad * centred, axis=-1, keepdims=True)))
                router_piece = lax.dot_general(normed, logit_grad, (((0,), (0,)), ((), ())), preferred_element_type=jnp.float32)
                return (input_grad.astype(jnp.bfloat16), router_piece, lax.optimization_barrier(jnp.sum(normed_grad * centred, axis=0)))
            operands = (saved_inputs[section_pos][micro_pos], saved_pairs[section_pos][micro_pos], grads_next[micro_pos])
            input_grad, router_piece, gain_piece = backward_layer(operands)
            router_sum = router_sum + router_piece
            gain_sum = gain_sum + gain_piece
            section_rows.append(input_grad)
            grads_next[micro_pos] = input_grad
        section_list[section_pos] = jnp.stack(section_rows, axis=0)
        router_list[section_pos] = router_sum / denominator
        gain_list[section_pos] = gain_sum / denominator
    return (jnp.stack(section_list, axis=0), jnp.stack(router_list, axis=0), jnp.stack(gain_list, axis=0))
```

```python
import jax
import jax.numpy as jnp
from jax import lax
from jax.sharding import PartitionSpec as P

EPSILON = 1e-06


def shifted(block, axis, distance):
    devices = range(lax.axis_size(axis))
    route = [(i - distance, i) for i in devices if i - distance in devices]
    return lax.ppermute(block, axis, route)


def normalize(hidden_in, gain_row):
    values = hidden_in.astype(jnp.float32)
    scale_inv = lax.rsqrt(jnp.mean(values * values, axis=-1, keepdims=True) + EPSILON)
    normed = (values * scale_inv * gain_row).astype(jnp.bfloat16)
    return (values, scale_inv, normed)


def expert_mix(row_block, weight_in):
    return jnp.dot(row_block, weight_in, preferred_element_type=jnp.float32)


def expert_apply(row_block, weight_in, weight_out):
    hidden = weight_out.shape[0]
    mixed_rows = expert_mix(row_block, weight_in)
    gate_part = mixed_rows[:, :hidden]
    up_part = mixed_rows[:, hidden:]
    activated = (gate_part * jax.nn.sigmoid(gate_part) * up_part).astype(jnp.bfloat16)
    result = jnp.dot(activated, weight_out, preferred_element_type=jnp.float32).astype(jnp.bfloat16)
    return (result, mixed_rows)


def expert_adjoint(mixed_rows, grad_rows, weight_in, weight_out):
    hidden = weight_out.shape[0]
    gate_part = mixed_rows[:, :hidden]
    up_part = mixed_rows[:, hidden:]
    act_grad = lax.dot_general(
        grad_rows, weight_out, (((1,), (1,)), ((), ())), preferred_element_type=jnp.float32
    )
    sigmoid_gate = jax.nn.sigmoid(gate_part)
    gate_grad = act_grad * up_part * sigmoid_gate * (1.0 + gate_part * (1.0 - sigmoid_gate))
    up_grad = act_grad * gate_part * sigmoid_gate
    joined = jnp.concatenate([gate_grad, up_grad], axis=1).astype(jnp.bfloat16)
    return lax.dot_general(
        joined, weight_in, (((1,), (1,)), ((), ())), preferred_element_type=jnp.float32
    ).astype(jnp.bfloat16)


def choice_weights(normed, router_local, route_rows):
    experts = router_local.shape[1]
    logits = jnp.dot(normed, router_local, preferred_element_type=jnp.float32)
    expert_codes = lax.broadcasted_iota(jnp.int32, (1, 1, experts), 2)
    chosen = route_rows[:, :, None] == expert_codes
    picked = jnp.sum(jnp.where(chosen, logits[:, None, :], 0.0), axis=-1)
    weights = jax.nn.sigmoid(picked - picked[:, ::-1])
    return (chosen, weights)


def slot_tables(chosen, live_rows, capacity):
    tokens_here, choice_count, experts = chosen.shape
    marked = (
        (chosen & live_rows[:, None, None])
        .reshape(tokens_here * choice_count, experts)
        .astype(jnp.int32)
    )
    earlier = jnp.cumsum(marked, axis=0) - marked
    position = jnp.sum(earlier * marked, axis=1)
    expert_codes = lax.broadcasted_iota(jnp.int32, (1, experts), 1)
    target = jnp.sum(marked * expert_codes, axis=1)
    present = jnp.sum(marked, axis=1) > 0
    slot_of = jnp.where(present, target * capacity + position, -1).reshape(
        tokens_here, choice_count
    )
    slot_codes = lax.broadcasted_iota(jnp.int32, (choice_count, experts * capacity, tokens_here), 1)
    return (jnp.transpose(slot_of)[:, None, :] == slot_codes).astype(jnp.bfloat16)


def store_at(buffer, new_value, slot_index, keep_flag):
    previous = lax.dynamic_index_in_dim(buffer, slot_index, 0, keepdims=False)
    return lax.dynamic_update_index_in_dim(
        buffer, jnp.where(keep_flag, new_value, previous), slot_index, 0
    )


def local(inputs, cotangent, lengths, norm_gain, router, expert_in, expert_out, routes):
    micro_count, tokens_here, model_width = inputs.shape
    sections = lax.axis_size("section")
    section_id = lax.axis_index("section")
    router_local = router[0]
    experts = router_local.shape[1]
    choice_count = routes.shape[3]
    capacity = choice_count * tokens_here // experts
    gain_row = norm_gain[0]
    weight_in = expert_in[0, 0]
    weight_out = expert_out[0, 0]
    hidden = weight_out.shape[0]
    positions = lax.broadcasted_iota(jnp.int32, (micro_count, tokens_here), 1)
    live_all = positions < lengths
    route_all = routes[0]
    ticks = sections + micro_count - 1
    inbox_rows = jnp.zeros((tokens_here, model_width), jnp.bfloat16)
    stored_inputs = jnp.zeros((micro_count, tokens_here, model_width), jnp.bfloat16)
    stored_outputs = jnp.zeros((micro_count, choice_count, tokens_here, model_width), jnp.float32)
    stored_mixed = jnp.zeros((micro_count, experts, capacity, 2 * hidden), jnp.float32)
    for tick_index in range(ticks):
        micro_index = tick_index - section_id
        inside = (micro_index >= 0) & (micro_index < micro_count)
        working = inside
        clipped = jnp.clip(micro_index, 0, micro_count - 1)
        arriving = lax.dynamic_index_in_dim(inputs, clipped, 0, keepdims=False)
        hidden_in = jnp.where(section_id == 0, arriving, inbox_rows)
        values, scale_inv, normed = normalize(hidden_in, gain_row)
        route_rows = lax.dynamic_index_in_dim(route_all, clipped, 0, keepdims=False)
        live_rows = lax.dynamic_index_in_dim(live_all, clipped, 0, keepdims=False)
        chosen, weights = choice_weights(normed, router_local, route_rows)
        pair_table = slot_tables(chosen, live_rows, capacity)
        slot_table = jnp.sum(pair_table, axis=0)
        outgoing = jnp.dot(slot_table, normed, preferred_element_type=jnp.float32).astype(
            jnp.bfloat16
        )
        outgoing = outgoing.reshape(experts, capacity, model_width)
        run_received = lax.all_to_all(outgoing, "expert", split_axis=0, concat_axis=0, tiled=True)
        row_shape = run_received.shape

        def compute(row_block):
            return expert_apply(row_block, weight_in, weight_out)

        def skip_work(row_block):
            return (
                jnp.zeros(row_block.shape, jnp.bfloat16),
                jnp.zeros((row_block.shape[0], 2 * hidden), jnp.float32),
            )

        run_result, mixed_rows = lax.cond(
            working, compute, skip_work, run_received.reshape(-1, model_width)
        )
        returned = lax.all_to_all(
            run_result.reshape(row_shape), "expert", split_axis=0, concat_axis=0, tiled=True
        )
        returned, mixed_rows = (
            returned,
            mixed_rows.reshape(row_shape[0], row_shape[1], 2 * hidden),
        )
        expert_rows = returned.reshape(experts * capacity, model_width)
        per_choice = jnp.einsum(
            "kst,sd->ktd", pair_table, expert_rows, preferred_element_type=jnp.float32
        )
        combined = jnp.sum(jnp.transpose(weights)[:, :, None] * per_choice, axis=0)
        leaving = (values + combined).astype(jnp.bfloat16)
        stored_inputs = store_at(stored_inputs, hidden_in, clipped, inside)
        stored_outputs = store_at(stored_outputs, per_choice, clipped, inside)
        stored_mixed = store_at(stored_mixed, mixed_rows, clipped, inside)
        inbox_rows = shifted(leaving, "section", 1)
    inbox_rows = jnp.zeros((tokens_here, model_width), jnp.bfloat16)
    router_total = jnp.zeros((model_width, experts), jnp.float32)
    gain_total = jnp.zeros((model_width,), jnp.float32)
    grads_out = jnp.zeros((micro_count, tokens_here, model_width), jnp.bfloat16)
    for tick_index in range(ticks):
        micro_index = tick_index - (sections - 1 - section_id)
        inside = (micro_index >= 0) & (micro_index < micro_count)
        working = inside
        clipped = jnp.clip(micro_index, 0, micro_count - 1)
        arriving = lax.dynamic_index_in_dim(cotangent, clipped, 0, keepdims=False)
        grad_in = jnp.where(section_id == sections - 1, arriving, inbox_rows)
        grad_values = grad_in.astype(jnp.float32)
        hidden_in = lax.dynamic_index_in_dim(stored_inputs, clipped, 0, keepdims=False)
        values, scale_inv, normed = normalize(hidden_in, gain_row)
        route_rows = lax.dynamic_index_in_dim(route_all, clipped, 0, keepdims=False)
        live_rows = lax.dynamic_index_in_dim(live_all, clipped, 0, keepdims=False)
        chosen, weights = choice_weights(normed, router_local, route_rows)
        pair_table = slot_tables(chosen, live_rows, capacity)
        per_choice = lax.dynamic_index_in_dim(stored_outputs, clipped, 0, keepdims=False)
        choice_grad = jnp.sum(grad_values[None] * per_choice, axis=-1)
        first_grad = weights[:, 0] * weights[:, 1] * (choice_grad[0] - choice_grad[1])
        pick_grad = jnp.stack([first_grad, -first_grad], axis=1)
        logit_grad = jnp.sum(jnp.where(chosen, pick_grad[:, :, None], 0.0), axis=1).astype(
            jnp.bfloat16
        )
        output_grad = (jnp.transpose(weights)[:, :, None] * grad_values[None]).astype(jnp.bfloat16)
        grad_send = jnp.einsum(
            "kst,ktd->sd", pair_table, output_grad, preferred_element_type=jnp.float32
        )
        grad_send = grad_send.astype(jnp.bfloat16).reshape(experts, capacity, model_width)
        received = lax.all_to_all(grad_send, "expert", split_axis=0, concat_axis=0, tiled=True)
        mixed_flat = lax.dynamic_index_in_dim(stored_mixed, clipped, 0, keepdims=False).reshape(
            -1, 2 * hidden
        )

        def compute_kept(packed):
            return expert_adjoint(packed[0], packed[1], weight_in, weight_out)

        def skip_kept(packed):
            return jnp.zeros(packed[1].shape, jnp.bfloat16)

        result = lax.cond(
            working, compute_kept, skip_kept, (mixed_flat, received.reshape(-1, model_width))
        )
        returned = lax.all_to_all(
            result.reshape(received.shape), "expert", split_axis=0, concat_axis=0, tiled=True
        )
        rows_back = returned.reshape(experts * capacity, model_width)
        normed_grad = jnp.sum(
            jnp.einsum("kst,sd->ktd", pair_table, rows_back, preferred_element_type=jnp.float32),
            axis=0,
        )
        normed_grad = normed_grad + lax.dot_general(
            logit_grad, router_local, (((1,), (1,)), ((), ())), preferred_element_type=jnp.float32
        )
        centred = values * scale_inv
        scaled_grad = normed_grad * gain_row
        input_grad = grad_values + scale_inv * (
            scaled_grad - centred * jnp.mean(scaled_grad * centred, axis=-1, keepdims=True)
        )
        leaving = input_grad.astype(jnp.bfloat16)
        router_piece = lax.dot_general(
            normed, logit_grad, (((0,), (0,)), ((), ())), preferred_element_type=jnp.float32
        )
        router_total = router_total + jnp.where(working, router_piece, 0.0)
        gain_total = gain_total + jnp.where(working, jnp.sum(normed_grad * centred, axis=0), 0.0)
        grads_out = store_at(grads_out, leaving, clipped, inside)
        inbox_rows = shifted(leaving, "section", -1)
    owners = lax.axis_size("expert")
    pieces = jnp.concatenate(
        [router_total.reshape(owners, -1), gain_total.reshape(owners, -1)], axis=1
    )
    pieces = lax.all_to_all(pieces, "expert", split_axis=0, concat_axis=0, tiled=True)
    piece = jnp.broadcast_to(jnp.sum(pieces, axis=0)[None], pieces.shape)
    pieces = lax.all_to_all(piece, "expert", split_axis=0, concat_axis=0, tiled=True)
    split = model_width * experts // owners
    router_sum = pieces[:, :split].reshape(model_width, experts)
    gain_sum = pieces[:, split:].reshape(model_width)
    denominator = micro_count * choice_count * tokens_here
    return (grads_out[None], (router_sum / denominator)[None], (gain_sum / denominator)[None])


def solution(mesh):
    in_specs = (
        P(None, "expert", None),
        P(None, "expert", None),
        P(None, "expert"),
        P("section", None),
        P("section", None, None),
        P("section", "expert", None, None),
        P("section", "expert", None, None),
        P("section", None, "expert", None),
    )
    out_specs = (P("section", None, "expert", None), P("section", None, None), P("section", None))
    return jax.shard_map(local, mesh=mesh, in_specs=in_specs, out_specs=out_specs, check_vma=False)
```

```python
import functools

import jax
import jax.numpy as jnp
from jax import lax
from jax.experimental import pallas as pl
from jax.experimental.pallas import tpu as pltpu
from jax.sharding import PartitionSpec as P

EPSILON = 1e-06
CHUNKS = 2
MESH = pl.DeviceIdType.MESH
F32 = jnp.float32
BF16 = jnp.bfloat16


def dot_nn(left, right):
    return jnp.dot(left, right, preferred_element_type=F32)


def dot_nt(left, right):
    return lax.dot_general(left, right, (((1,), (1,)), ((), ())), preferred_element_type=F32)


def dot_tn(left, right):
    return lax.dot_general(left, right, (((0,), (0,)), ((), ())), preferred_element_type=F32)


def wait_bytes(ref, sem):
    pltpu.make_async_copy(ref, ref, sem).wait()


def peer_of(me, step, experts):
    if experts != 64:
        return lax.rem(me + step + 1, experts)
    far, near = step // 8, lax.rem(step + 1, 8)
    half = (far + 1) // 2
    shift_z = 4 + half * (1 - 2 * lax.rem(far, 2))
    my_z, my_y, my_core = me // 8, lax.rem(me // 2, 4), lax.rem(me, 2)
    to_z = lax.rem(my_z + shift_z, 8)
    to_y = lax.rem(my_y + near // 2, 4)
    to_core = lax.rem(my_core + lax.rem(near, 2), 2)
    return (to_z * 4 + to_y) * 2 + to_core


def kernel(
    experts, sections, denominator,
    inputs, cotangent, lengths, gain, router, w_in_hbm, w_out_hbm, routes,
    grads_out, router_out, gain_out,
    w_in, w_out, h_in, h_out, d_in, d_out,
    x_send, x_recv, y_send, y_recv, g_send, g_recv, r_send, r_recv, p_send, p_recv,
    f_send, f_recv, mixed, joined, q_keep, take, give, stats, logit_keep, column, gain_part,
    weight_sem, out_sem, h_sem, d_sem, x_sem, y_sem, g_sem, r_sem, p_sem, f_sem,
    xs_sem, ys_sem, gs_sem, rs_sem, ps_sem, fs_sem, hs_sem, ds_sem,
):
    section = lax.axis_index("section")
    me = lax.axis_index("expert")
    micros, tokens, width = inputs.shape
    hidden = w_out.shape[0]
    slots = 2 * experts
    piece = width // CHUNKS
    chunk_ids = range(CHUNKS)

    def cols(index):
        return pl.ds(index * piece, piece)

    load_in = pltpu.make_async_copy(w_in_hbm.at[0, 0], w_in, weight_sem.at[0])
    load_out = pltpu.make_async_copy(w_out_hbm.at[0, 0], w_out, weight_sem.at[1])

    @pl.when(section == 0)
    def _():
        for m in range(micros):
            for c in chunk_ids:
                pltpu.make_async_copy(inputs.at[m, :, cols(c)], h_in.at[m, c], h_sem.at[m, c]).start()

    load_in.start()
    load_out.start()

    @pl.when(section == sections - 1)
    def _():
        for m in range(micros):
            for c in chunk_ids:
                pltpu.make_async_copy(cotangent.at[m, :, cols(c)], d_in.at[m, c], d_sem.at[m, c]).start()

    barrier = pltpu.get_barrier_semaphore()

    def greet(step, carry):
        pl.semaphore_signal(barrier, inc=1, device_id={"expert": peer_of(me, step, experts)}, device_id_type=MESH)
        return carry

    lax.fori_loop(0, experts - 1, greet, 0)

    @pl.when(section > 0)
    def _():
        pl.semaphore_signal(barrier, inc=1, device_id={"section": section - 1}, device_id_type=MESH)

    @pl.when(section < sections - 1)
    def _():
        pl.semaphore_signal(barrier, inc=1, device_id={"section": section + 1}, device_id_type=MESH)

    column[...] = jnp.zeros_like(column)
    gain_part[...] = jnp.zeros_like(gain_part)
    expert_codes = lax.broadcasted_iota(jnp.int32, (tokens, experts), 1)

    def chosen_of(m, k):
        return routes[0, m][:, k : k + 1] == expert_codes

    earlier = (
        lax.broadcasted_iota(jnp.int32, (tokens, tokens), 1)
        < lax.broadcasted_iota(jnp.int32, (tokens, tokens), 0)
    ).astype(F32).astype(BF16)
    slot_codes = lax.broadcasted_iota(jnp.int32, (tokens, slots), 1).astype(F32)
    positions = lax.broadcasted_iota(jnp.int32, (tokens, 1), 0)
    for m in range(micros):
        live = positions < lengths[m : m + 1, :]
        tables = []
        for k in range(2):
            marked = chosen_of(m, k).astype(F32)
            rank = jnp.sum(marked * dot_nn(earlier, marked.astype(BF16)), axis=1, keepdims=True)
            slot = routes[0, m][:, k : k + 1].astype(F32) * 2.0 + rank
            tables.append(((slot == slot_codes) & live).astype(F32))
        table = jnp.concatenate(tables, axis=0)
        give[m] = table.astype(BF16)
        take[m] = table.T.astype(BF16)

    pl.semaphore_wait(
        barrier,
        experts - 1 + (section > 0).astype(jnp.int32) + (section < sections - 1).astype(jnp.int32),
    )

    def scatter(source, target, send_sem, recv_sem):
        pltpu.make_async_copy(source(me), target, recv_sem).start()

        def one(step, carry):
            peer = peer_of(me, step, experts)
            pltpu.make_async_remote_copy(
                src_ref=source(peer), dst_ref=target, send_sem=send_sem, recv_sem=recv_sem,
                device_id={"expert": peer}, device_id_type=MESH,
            ).start()
            return carry

        lax.fori_loop(0, experts - 1, one, 0)

    def exchange(m, c, values, sends, receives, send_sem, recv_sem):
        sends[m, :, :, cols(c)] = values.astype(BF16).reshape(experts, 2, piece)
        scatter(
            lambda peer: sends.at[m, peer, :, cols(c)], receives.at[m, me, :, cols(c)],
            send_sem.at[m, c], recv_sem.at[m, c],
        )

    def rows_of(buffer, m, c):
        return buffer[m, :, :, cols(c)].reshape(slots, piece)

    def values_of(m, c):
        return h_in[m, c].astype(F32)

    def gain_of(c):
        return gain[:, c * piece : (c + 1) * piece]

    def forward(m, carry):
        square = jnp.zeros((tokens, 1), F32)
        for c in chunk_ids:
            wait_bytes(h_in.at[m, c], h_sem.at[m, c])
            values = values_of(m, c)
            square += jnp.sum(values * values, axis=1, keepdims=True)
        scale = lax.rsqrt(square / width + EPSILON)
        logits = jnp.zeros((tokens, experts), F32)
        for c in chunk_ids:
            normed = (values_of(m, c) * scale * gain_of(c)).astype(BF16)
            exchange(m, c, dot_nn(take[m], jnp.concatenate([normed, normed], axis=0)), x_send, x_recv, xs_sem, x_sem)
            logits += dot_nn(normed, router[0, c * piece : (c + 1) * piece, :])
        picked = [
            jnp.sum(jnp.where(chosen_of(m, k), logits, 0.0), axis=1, keepdims=True) for k in range(2)
        ]
        first, second = jax.nn.sigmoid(picked[0] - picked[1]), jax.nn.sigmoid(picked[1] - picked[0])
        for index, stat in enumerate((scale, first, second)):
            stats[m, index] = jnp.broadcast_to(stat, (tokens, 128))

        @pl.when(m == 0)
        def _():
            load_in.wait()
            load_out.wait()

        for c in chunk_ids:
            wait_bytes(x_recv.at[m, :, :, cols(c)], x_sem.at[m, c])
            part = dot_nn(rows_of(x_recv, m, c), w_in[c * piece : (c + 1) * piece, :])
            mixed[m] = part if c == 0 else mixed[m] + part
        gate, up = mixed[m, :, :hidden], mixed[m, :, hidden:]
        activated = (gate * jax.nn.sigmoid(gate) * up).astype(BF16)
        for c in chunk_ids:
            exchange(m, c, dot_nn(activated, w_out[:, c * piece : (c + 1) * piece]), y_send, y_recv, ys_sem, y_sem)
        for c in chunk_ids:
            wait_bytes(y_recv.at[m, :, :, cols(c)], y_sem.at[m, c])
            per_choice = dot_nn(give[m], rows_of(y_recv, m, c))
            combined = first * per_choice[:tokens] + second * per_choice[tokens:]
            h_out[m, c] = (values_of(m, c) + combined).astype(BF16)

            @pl.when(section < sections - 1)
            def _():
                pltpu.make_async_remote_copy(
                    src_ref=h_out.at[m, c], dst_ref=h_in.at[m, c], send_sem=hs_sem.at[m, c],
                    recv_sem=h_sem.at[m, c], device_id={"section": section + 1}, device_id_type=MESH,
                ).start()

        return carry

    lax.fori_loop(0, micros, forward, 0)

    def backward(m, carry):
        scale, first, second = (stats[m, index][:, :1] for index in range(3))
        for c in chunk_ids:
            wait_bytes(d_in.at[m, c], d_sem.at[m, c])
            grad = d_in[m, c].astype(F32)
            pair = jnp.concatenate([(first * grad).astype(BF16), (second * grad).astype(BF16)], axis=0)
            exchange(m, c, dot_nn(take[m], pair), g_send, g_recv, gs_sem, g_sem)
        difference = jnp.zeros((tokens, 1), F32)
        for c in chunk_ids:
            per_choice = dot_nn(give[m], rows_of(y_recv, m, c))
            grad = d_in[m, c].astype(F32)
            difference += jnp.sum(grad * per_choice[:tokens], axis=1, keepdims=True) - jnp.sum(
                grad * per_choice[tokens:], axis=1, keepdims=True
            )
        pick = first * second * difference
        picks = jnp.concatenate([pick, -pick], axis=0)
        lanes = lax.broadcasted_iota(jnp.int32, (2 * tokens, 128), 1)
        picks = jnp.where(lanes == 0, picks, 0.0).astype(BF16)
        p_send[m] = dot_nn(take[m], picks).astype(BF16).reshape(experts, 2, 128)
        scatter(lambda peer: p_send.at[m, peer], p_recv.at[m, me], ps_sem.at[m], p_sem.at[m])
        logit_grad = jnp.where(chosen_of(m, 0), pick, 0.0) + jnp.where(chosen_of(m, 1), -pick, 0.0)
        logit_keep[...] = logit_grad.astype(BF16)

        for c in chunk_ids:
            wait_bytes(g_recv.at[m, :, :, cols(c)], g_sem.at[m, c])
            part = dot_nt(rows_of(g_recv, m, c), w_out[:, c * piece : (c + 1) * piece])
            act_grad = part if c == 0 else act_grad + part
        gate, up = mixed[m, :, :hidden], mixed[m, :, hidden:]
        sigmoid_gate = jax.nn.sigmoid(gate)
        joined[:, :hidden] = (act_grad * up * sigmoid_gate * (1.0 + gate * (1.0 - sigmoid_gate))).astype(BF16)
        joined[:, hidden:] = (act_grad * gate * sigmoid_gate).astype(BF16)
        for c in chunk_ids:
            exchange(m, c, dot_nt(joined[...], w_in[c * piece : (c + 1) * piece, :]), r_send, r_recv, rs_sem, r_sem)
        wait_bytes(p_recv.at[m], p_sem.at[m])
        pick_rows = p_recv[m].reshape(slots, 128)
        for c in chunk_ids:
            rows = rows_of(x_recv, m, c)
            column[:, cols(c)] += dot_tn(pick_rows, rows)[:1]
            row_grads = rows_of(r_send, m, c).astype(F32)
            gain_part[:, cols(c)] += jnp.sum(row_grads * rows.astype(F32), axis=0, keepdims=True)

        @pl.when(m == micros - 1)
        def _():
            mine = (lax.broadcasted_iota(jnp.int32, (8, experts), 1) == me).astype(F32).astype(BF16)
            own_router = dot_nt(mine, router[0])[:1]
            f_send[0] = jnp.concatenate(
                [column[...], (gain_part[...] + own_router * column[...]) / gain[...]], axis=0
            )
            scatter(lambda peer: f_send.at[0], f_recv.at[me], fs_sem, f_sem)

        both = give[m, :tokens] + give[m, tokens:]
        inner = jnp.zeros((tokens, 1), F32)
        for c in chunk_ids:
            base = dot_nt(logit_keep[...], router[0, c * piece : (c + 1) * piece, :])
            wait_bytes(r_recv.at[m, :, :, cols(c)], r_sem.at[m, c])
            scaled = (dot_nn(both, rows_of(r_recv, m, c)) + base) * gain_of(c)
            q_keep[:, cols(c)] = scaled
            inner += jnp.sum(scaled * (values_of(m, c) * scale), axis=1, keepdims=True)
        inner = inner / width
        for c in chunk_ids:
            centred = values_of(m, c) * scale
            grad = d_in[m, c].astype(F32)
            d_out[m, c] = (grad + scale * (q_keep[:, cols(c)] - centred * inner)).astype(BF16)

            @pl.when(section > 0)
            def _():
                pltpu.make_async_remote_copy(
                    src_ref=d_out.at[m, c], dst_ref=d_in.at[m, c], send_sem=ds_sem.at[m, c],
                    recv_sem=d_sem.at[m, c], device_id={"section": section - 1}, device_id_type=MESH,
                ).start()

            pltpu.make_async_copy(d_out.at[m, c], grads_out.at[0, m, :, cols(c)], out_sem.at[m, c]).start()
        return carry

    lax.fori_loop(0, micros, backward, 0)

    wait_bytes(f_recv, f_sem)
    router_out[...] = f_recv[:, 0, :] / denominator
    gain_out[...] = jnp.sum(f_recv[:, 1, :], axis=0, keepdims=True) / denominator

    others = pl.ds(0, experts - 1)

    def drain(m, carry):
        for c in chunk_ids:
            for buffer, sem in ((x_send, xs_sem), (y_send, ys_sem), (g_send, gs_sem), (r_send, rs_sem)):
                wait_bytes(buffer.at[m, others, :, cols(c)], sem.at[m, c])
            wait_bytes(d_out.at[m, c], out_sem.at[m, c])

            @pl.when(section < sections - 1)
            def _():
                wait_bytes(h_out.at[m, c], hs_sem.at[m, c])

            @pl.when(section > 0)
            def _():
                wait_bytes(d_out.at[m, c], ds_sem.at[m, c])

        wait_bytes(p_send.at[m, others], ps_sem.at[m])
        return carry

    lax.fori_loop(0, micros, drain, 0)
    wait_bytes(f_recv.at[others], fs_sem)


def solution(mesh):
    sections, experts = mesh.shape["section"], mesh.shape["expert"]

    def local(inputs, cotangent, lengths, norm_gain, router, expert_in, expert_out, routes):
        micros, tokens, width = inputs.shape
        hidden = expert_out.shape[2]
        piece = width // CHUNKS
        vmem = pl.BlockSpec(memory_space=pltpu.VMEM)
        hbm = pl.BlockSpec(memory_space=pl.ANY)
        DMA = pltpu.SemaphoreType.DMA
        plane = pltpu.VMEM((micros, CHUNKS, tokens, piece), BF16)
        slab = pltpu.VMEM((micros, experts, 2, width), BF16)
        small = pltpu.VMEM((micros, experts, 2, 128), BF16)
        each = DMA((micros, CHUNKS))
        grads, router_rows, gain_row = pl.pallas_call(
            functools.partial(kernel, experts, sections, float(micros * 2 * tokens)),
            out_shape=(
                jax.ShapeDtypeStruct((1, micros, tokens, width), BF16),
                jax.ShapeDtypeStruct((experts, width), F32),
                jax.ShapeDtypeStruct((1, width), F32),
            ),
            in_specs=[hbm, hbm, vmem, vmem, vmem, hbm, hbm, vmem],
            out_specs=(hbm, vmem, vmem),
            scratch_shapes=[
                pltpu.VMEM((width, 2 * hidden), BF16),
                pltpu.VMEM((hidden, width), BF16),
                plane, plane, plane, plane,
                slab, slab, slab, slab, slab, slab, slab, slab, small, small,
                pltpu.VMEM((1, 2, width), F32),
                pltpu.VMEM((experts, 2, width), F32),
                pltpu.VMEM((micros, 2 * experts, 2 * hidden), F32),
                pltpu.VMEM((2 * experts, 2 * hidden), BF16),
                pltpu.VMEM((tokens, width), F32),
                pltpu.VMEM((micros, 2 * experts, 2 * tokens), BF16),
                pltpu.VMEM((micros, 2 * tokens, 2 * experts), BF16),
                pltpu.VMEM((micros, 3, tokens, 128), F32),
                pltpu.VMEM((tokens, experts), BF16),
                pltpu.VMEM((1, width), F32),
                pltpu.VMEM((1, width), F32),
                DMA((2,)), each, each, each, each, each, each, each, DMA((micros,)), DMA,
                each, each, each, each, DMA((micros,)), DMA, each, each,
            ],
            compiler_params=pltpu.CompilerParams(
                collective_id=0, has_side_effects=True, vmem_limit_bytes=60 * 1024 * 1024
            ),
        )(inputs, cotangent, lengths, norm_gain, router, expert_in, expert_out, routes)
        return grads, router_rows.T[None], gain_row

    in_specs = (
        P(None, "expert", None),
        P(None, "expert", None),
        P(None, "expert"),
        P("section", None),
        P("section", None, None),
        P("section", "expert", None, None),
        P("section", "expert", None, None),
        P("section", None, "expert", None),
    )
    out_specs = (P("section", None, "expert", None), P("section", None, None), P("section", None))
    return jax.shard_map(local, mesh=mesh, in_specs=in_specs, out_specs=out_specs, check_vma=False)
```

```python
import functools

import jax
import jax.numpy as jnp
from jax import lax
from jax.experimental import pallas as pl
from jax.experimental.pallas import tpu as pltpu
from jax.sharding import PartitionSpec as P

EPSILON = 1e-06
MESH = pl.DeviceIdType.MESH
F32 = jnp.float32
BF16 = jnp.bfloat16


def dot_nn(left, right):
    return jnp.dot(left, right, preferred_element_type=F32)


def dot_nt(left, right):
    return lax.dot_general(left, right, (((1,), (1,)), ((), ())), preferred_element_type=F32)


def dot_tn(left, right):
    return lax.dot_general(left, right, (((0,), (0,)), ((), ())), preferred_element_type=F32)


def wait_bytes(ref, sem):
    pltpu.make_async_copy(ref, ref, sem).wait()


def for_peers(me, experts, visit):
    if experts != 64:
        for step in range(1, experts):
            visit(lax.rem(me + step, experts))
        return
    my_z, my_y, my_core = me // 8, lax.rem(me // 2, 4), lax.rem(me, 2)
    near = [lax.rem(my_y + q // 2, 4) * 2 + lax.rem(my_core + q % 2, 2) for q in range(8)]

    def ring(step, carry):
        half = (step + 1) // 2
        base = lax.rem(my_z + 4 + half * (1 - 2 * lax.rem(step, 2)), 8) * 8
        for q in range(8):
            visit(base + near[q])
        return carry

    lax.fori_loop(0, 7, ring, 0)
    for q in range(1, 8):
        visit(my_z * 8 + near[q])


def column_of(wide):
    return wide[:, :1]


def kernel(
    experts, denominator,
    inputs, cotangent, lengths, gain, router, w_in_hbm, w_out_hbm, routes,
    grads_out, router_out, gain_out,
    w_in, w_out, hidden_of, grad_of, give, router_send, router_of, gain_send, gain_of,
    x_send, x_recv, y_send, y_relay, y_recv, g_send, g_recv, r_send, r_relay, r_recv,
    p_send, p_recv, f_send, f_recv, s_send, s_recv, t_send, t_recv,
    norm_send, norm_recv, diff_send, diff_recv, inner_send, inner_recv, norm_keep,
    mixed, joined, q_keep, row_scale, logit_keep, column, gain_part,
    plane_sem, weight_sem, h_sem, c_sem, give_sem, router_sem, gain_sem,
    x_sem, yr_sem, y_sem, g_sem, rr_sem, r_sem, p_sem, f_sem, s_sem, t_sem,
    norm_sem, diff_sem, inner_sem, o_sem,
    give_ss, router_ss, gain_ss, x_ss, yr_ss, y_ss, g_ss, rr_ss, r_ss, p_ss, f_ss, s_ss, t_ss,
    norm_ss, diff_ss, inner_ss, o_ss,
):
    x = lax.axis_index("section")
    me = lax.axis_index("expert")
    micros, tokens, width = inputs.shape
    sections = 4
    hidden = w_out.shape[1]
    slots = 2 * experts
    piece = width // sections
    owners = s_send.shape[0]
    stride = experts // owners
    ms = range(micros)

    def cols(q):
        return pl.ds(pl.multiple_of(q * piece, piece), piece)

    def send(source, target, send_sem, recv_sem, section, expert):
        pltpu.make_async_remote_copy(
            src_ref=source, dst_ref=target, send_sem=send_sem, recv_sem=recv_sem,
            device_id={"section": section, "expert": expert}, device_id_type=MESH,
        ).start()

    for m in ms:
        pltpu.make_async_copy(inputs.at[m, :, cols(x)], hidden_of.at[0, m], h_sem.at[m]).start()
    loads = []
    for q in range(sections):
        loads.append(pltpu.make_async_copy(w_in_hbm.at[0, 0, pl.ds(q * piece, piece)], w_in.at[q], weight_sem.at[0, q]))
    for q in range(sections):
        loads.append(pltpu.make_async_copy(w_out_hbm.at[0, 0, :, pl.ds(q * piece, piece)], w_out.at[q], weight_sem.at[1, q]))
    for load in loads:
        load.start()
    for m in ms:
        pltpu.make_async_copy(cotangent.at[m, :, cols(x)], grad_of.at[sections, m], c_sem.at[m]).start()

    barrier = pltpu.get_barrier_semaphore()

    def greet(peer):
        pl.semaphore_signal(barrier, inc=1, device_id={"section": x, "expert": peer}, device_id_type=MESH)

    for_peers(me, experts, greet)
    others = [lax.rem(x + step, sections) for step in (1, 3, 2)]
    for other in others:
        pl.semaphore_signal(barrier, inc=1, device_id={"section": other, "expert": me}, device_id_type=MESH)

    column[...] = jnp.zeros_like(column)
    gain_part[...] = jnp.zeros_like(gain_part)
    expert_codes = lax.broadcasted_iota(jnp.int32, (tokens, experts), 1)
    earlier = (
        lax.broadcasted_iota(jnp.int32, (tokens, tokens), 1)
        < lax.broadcasted_iota(jnp.int32, (tokens, tokens), 0)
    ).astype(F32).astype(BF16)
    slot_codes = lax.broadcasted_iota(jnp.int32, (tokens, slots), 1).astype(F32)
    positions = lax.broadcasted_iota(jnp.int32, (tokens, 1), 0)
    for m in ms:
        live = positions < lengths[m : m + 1, :]
        tables = []
        for k in range(2):
            choice = routes[0, m][:, k : k + 1]
            marked = (choice == expert_codes).astype(F32)
            rank = jnp.sum(marked * dot_nn(earlier, marked.astype(BF16)), axis=1, keepdims=True)
            slot = choice.astype(F32) * 2.0 + rank
            tables.append(((slot == slot_codes) & live).astype(F32))
        give[x, m] = jnp.concatenate(tables, axis=0).astype(BF16)
    eye = (
        lax.broadcasted_iota(jnp.int32, (experts, experts), 0)
        == lax.broadcasted_iota(jnp.int32, (experts, experts), 1)
    ).astype(F32).astype(BF16)
    for q in range(sections):
        router_send[q] = dot_nt(eye, router[0, q * piece : (q + 1) * piece, :]).astype(BF16)
        gain_send[q] = gain[:, q * piece : (q + 1) * piece]
    router_of[x] = router_send[x]
    gain_of[x] = gain_send[x]
    fold = (
        lax.broadcasted_iota(jnp.int32, (slots, experts), 0) // 2
        == lax.broadcasted_iota(jnp.int32, (slots, experts), 1)
    ).astype(F32).astype(BF16)

    pl.semaphore_wait(barrier, experts - 1 + sections - 1)
    for other in others:
        pl.semaphore_signal(plane_sem, inc=1, device_id={"section": other, "expert": me}, device_id_type=MESH)
    for other in others:
        send(gain_send.at[other], gain_of.at[x], gain_ss, gain_sem.at[x], other, me)
        send(give.at[x], give.at[x], give_ss, give_sem.at[x], other, me)
        send(router_send.at[other], router_of.at[x], router_ss, router_sem.at[x], other, me)
    pl.semaphore_wait(plane_sem, sections - 1)

    def share(values, sends, receives, send_sem, recv_sem, j, m):
        sends[j, m] = values
        for slot, other in enumerate(others):
            send(sends.at[j, m], receives.at[j, m, slot], send_sem.at[j, m], recv_sem.at[j, m], other, me)

    def shared(sends, receives, recv_sem, j, m):
        wait_bytes(receives.at[j, m], recv_sem.at[j, m])
        return sends[j, m] + receives[j, m, 0] + receives[j, m, 1] + receives[j, m, 2]

    def wide(values):
        return jnp.broadcast_to(values, (tokens, 128))

    def signs(j, m):
        return dot_nn(give[j, m, :tokens] - give[j, m, tokens:], fold)

    def scales(j, m):
        total = norm_keep[j, m]
        scale = lax.rsqrt(total[:, 0:1] / width + EPSILON)
        margin = total[:, 1:2] * scale
        return scale, jax.nn.sigmoid(margin), jax.nn.sigmoid(-margin)

    def dispatch(values, sends, receives, send_sem, recv_sem, j, m):
        sends[j, m] = dot_tn(give[j, m], values).astype(BF16).reshape(experts, 2, piece)
        target, arrive, leave = receives.at[m, x, me], recv_sem.at[m, x], send_sem.at[j, m]
        for_peers(me, experts, lambda peer: send(sends.at[j, m, peer], target, leave, arrive, j, peer))

        @pl.when(x == j)
        def _():
            pltpu.make_async_copy(sends.at[j, m, me], target, arrive).start()

        @pl.when(x != j)
        def _():
            send(sends.at[j, m, me], target, leave, arrive, j, me)

    def forward_send(j, m):
        values = hidden_of[j, m].astype(F32)
        rows = (values * gain_of[j]).astype(BF16)
        dispatch(jnp.concatenate([rows, rows], axis=0), x_send, x_recv, x_ss, x_sem, j, m)
        logits = dot_nt(rows, router_of[j])
        margin = jnp.sum(signs(j, m) * logits, axis=1, keepdims=True)
        square = jnp.sum(values * values, axis=1, keepdims=True)
        lanes = lax.broadcasted_iota(jnp.int32, (tokens, 128), 1)
        share(jnp.where(lanes == 0, square, jnp.where(lanes == 1, margin, 0.0)), norm_send, norm_recv, norm_ss, norm_sem, j, m)

    def settle(j, m):
        norm_keep[j, m] = shared(norm_send, norm_recv, norm_sem, j, m)

    def backward_send(j, m):
        _, first, second = scales(j, m)
        grad = grad_of[j + 1, m].astype(F32)
        pair = jnp.concatenate([(first * grad).astype(BF16), (second * grad).astype(BF16)], axis=0)
        dispatch(pair, g_send, g_recv, g_ss, g_sem, j, m)

    near_first = [lax.rem(x + step, sections) for step in (0, 1, 3, 2)]
    far_first = [lax.rem(x + step, sections) for step in (2, 1, 3)]

    def expert_forward(j, m):
        square = jnp.zeros((slots, 1), F32)
        for index, q in enumerate(near_first):
            wait_bytes(x_recv.at[m, q], x_sem.at[m, q])
            rows = x_recv[m, q].reshape(slots, piece)
            if m == 0:
                wait_bytes(w_in.at[q], weight_sem.at[0, q])
            part = dot_nn(rows, w_in[q])
            mixed[m] = part if index == 0 else mixed[m] + part
            plain = rows.astype(F32) / gain_send[q]
            square += jnp.sum(plain * plain, axis=1, keepdims=True)
        scale = lax.rsqrt(square / width + EPSILON)
        row_scale[m] = jnp.broadcast_to(scale, (slots, 128))
        gate, up = mixed[m, :, :hidden] * scale, mixed[m, :, hidden:] * scale
        mixed[m, :, :hidden] = gate
        mixed[m, :, hidden:] = up
        activated = (gate * jax.nn.sigmoid(gate) * up).astype(BF16)
        for q in far_first + [x]:
            if m == 0:
                wait_bytes(w_out.at[q], weight_sem.at[1, q])
            result = dot_nn(activated, w_out[q]).astype(BF16).reshape(experts, 2, piece)
            if q is x:
                y_relay[j, m] = result
            else:
                y_send[m, q] = result
                send(y_send.at[m, q], y_relay.at[j, m], yr_ss.at[m], yr_sem.at[j, m], q, me)

    def relay(buffer, target, bulk_sem, send_sem, recv_sem, j, m):
        @pl.when(x != j)
        def _():
            wait_bytes(buffer.at[j, m], bulk_sem.at[j, m])

        own = target.at[j, m, me]
        pltpu.make_async_copy(buffer.at[j, m, me], own, recv_sem.at[j, m]).start()
        for_peers(me, experts, lambda peer: send(buffer.at[j, m, peer], own, send_sem.at[j, m], recv_sem.at[j, m], x, peer))

    def choices(j, m):
        return dot_nn(give[j, m], y_recv[j, m].reshape(slots, piece))

    def forward_combine(j, m):
        wait_bytes(y_recv.at[j, m], y_sem.at[j, m])
        per_choice = choices(j, m)
        _, first, second = scales(j, m)
        combined = first * per_choice[:tokens] + second * per_choice[tokens:]
        hidden_of[j + 1, m] = (hidden_of[j, m].astype(F32) + combined).astype(BF16)

    def learn(j):
        @pl.when(x != j)
        def _():
            wait_bytes(gain_of.at[j], gain_sem.at[j])
            wait_bytes(give.at[j], give_sem.at[j])
            wait_bytes(router_of.at[j], router_sem.at[j])

    learn(0)
    for m in ms:
        wait_bytes(hidden_of.at[0, m], h_sem.at[m])
        forward_send(0, m)
    for m in ms:
        settle(0, m)

    def forward_stage(j, carry):
        for m in ms:
            @pl.when(x == j)
            def _():
                expert_forward(j, m)

            relay(y_relay, y_recv, yr_sem, y_ss, y_sem, j, m)

        @pl.when(j < sections - 1)
        def _():
            learn(j + 1)
            for m in ms:
                forward_combine(j, m)
                forward_send(j + 1, m)
            for m in ms:
                settle(j + 1, m)

        @pl.when(j == sections - 2)
        def _():
            for m in ms:
                wait_bytes(grad_of.at[sections, m], c_sem.at[m])
                backward_send(sections - 1, m)

        return carry

    lax.fori_loop(0, sections, forward_stage, 0)

    def expert_backward(j, m):
        for index, q in enumerate(near_first):
            wait_bytes(g_recv.at[m, q], g_sem.at[m, q])
            part = dot_nt(g_recv[m, q].reshape(slots, piece), w_out[q])
            act_grad = part if index == 0 else act_grad + part
        gate, up = mixed[m, :, :hidden], mixed[m, :, hidden:]
        sigmoid_gate = jax.nn.sigmoid(gate)
        joined[:, :hidden] = (act_grad * up * sigmoid_gate * (1.0 + gate * (1.0 - sigmoid_gate))).astype(BF16)
        joined[:, hidden:] = (act_grad * gate * sigmoid_gate).astype(BF16)
        for q in far_first + [x]:
            result = dot_nt(joined[...], w_in[q]).astype(BF16).reshape(experts, 2, piece)
            r_send[m, q] = result
            if q is x:
                r_relay[j, m] = result
            else:
                send(r_send.at[m, q], r_relay.at[j, m], rr_ss.at[m], rr_sem.at[j, m], q, me)

    def differ(j, m):
        @pl.when(j == sections - 1)
        def _():
            wait_bytes(y_recv.at[j, m], y_sem.at[j, m])

        per_choice = choices(j, m)
        grad = grad_of[j + 1, m].astype(F32)
        difference = jnp.sum(grad * (per_choice[:tokens] - per_choice[tokens:]), axis=1, keepdims=True)
        share(wide(difference), diff_send, diff_recv, diff_ss, diff_sem, j, m)

    def pick_choice(j, m):
        difference = column_of(shared(diff_send, diff_recv, diff_sem, j, m))
        _, first, second = scales(j, m)
        pick = first * second * difference
        logit_keep[m] = (pick * signs(j, m)).astype(BF16)

        @pl.when(x == j)
        def _():
            lanes = lax.broadcasted_iota(jnp.int32, (2 * tokens, 128), 1)
            picks = jnp.where(lanes == 0, jnp.concatenate([pick, -pick], axis=0), 0.0).astype(BF16)
            p_send[m] = dot_tn(give[j, m], picks).astype(BF16).reshape(experts, 2, 128)
            own = p_recv.at[m, me]
            pltpu.make_async_copy(p_send.at[m, me], own, p_sem.at[m]).start()
            for_peers(me, experts, lambda peer: send(p_send.at[m, peer], own, p_ss.at[m], p_sem.at[m], x, peer))

    def parameter_sums():
        for m in ms:
            wait_bytes(p_recv.at[m], p_sem.at[m])
            scale = column_of(row_scale[m])
            weight = p_recv[m].reshape(slots, 128)[:, :1].astype(F32) * scale
            for q in range(sections):
                rows = x_recv[m, q].reshape(slots, piece).astype(F32)
                row_grads = r_send[m, q].reshape(slots, piece).astype(F32)
                column[q] += jnp.sum(rows * weight, axis=0, keepdims=True)
                gain_part[q] += jnp.sum(row_grads * (rows * scale), axis=0, keepdims=True)
        mine = (lax.broadcasted_iota(jnp.int32, (8, experts), 1) == me).astype(F32).astype(BF16)
        for q in range(sections):
            own_router = dot_nn(mine, router_send[q])[:1]
            total = (gain_part[q] + own_router * column[q]) / gain_send[q]
            for b in range(owners // sections):
                s_send[q * (owners // sections) + b] = total[:, b * 128 : (b + 1) * 128]
        f_send[0] = jnp.concatenate(
            [jnp.concatenate([column[0], column[1]], axis=1), jnp.concatenate([column[2], column[3]], axis=1)], axis=0
        ).astype(BF16)
        for b in range(owners):
            @pl.when(me == b * stride)
            def _():
                pltpu.make_async_copy(s_send.at[b], s_recv.at[me], s_sem).start()

            @pl.when(me != b * stride)
            def _():
                send(s_send.at[b], s_recv.at[me], s_ss, s_sem, x, b * stride)

        pltpu.make_async_copy(f_send.at[0], f_recv.at[me], f_sem).start()
        for_peers(me, experts, lambda peer: send(f_send.at[0], f_recv.at[me], f_ss, f_sem, x, peer))

    def owner_sum():
        wait_bytes(s_recv, s_sem)
        t_send[0] = jnp.sum(s_recv[:, 0, :], axis=0, keepdims=True) / denominator
        own = t_recv.at[me // stride]
        pltpu.make_async_copy(t_send.at[0], own, t_sem).start()
        for_peers(me, experts, lambda peer: send(t_send.at[0], own, t_ss, t_sem, x, peer))

    def backward_gather(j, m):
        wait_bytes(r_recv.at[j, m], r_sem.at[j, m])
        both = give[j, m, :tokens] + give[j, m, tokens:]
        scaled = (
            dot_nn(both, r_recv[j, m].reshape(slots, piece)) + dot_nn(logit_keep[m], router_of[j])
        ) * gain_of[j]
        q_keep[m] = scaled
        scale, _, _ = scales(j, m)
        inner = jnp.sum(scaled * (hidden_of[j, m].astype(F32) * scale), axis=1, keepdims=True)
        share(wide(inner), inner_send, inner_recv, inner_ss, inner_sem, j, m)

    def backward_finish(j, m):
        scale, _, _ = scales(j, m)
        inner = column_of(shared(inner_send, inner_recv, inner_sem, j, m)) / width
        centred = hidden_of[j, m].astype(F32) * scale
        grad = grad_of[j + 1, m].astype(F32)
        grad_of[j, m] = (grad + scale * (q_keep[m] - centred * inner)).astype(BF16)

        @pl.when(j > 0)
        def _():
            backward_send(j - 1, m)

        target = grads_out.at[0, m, :, cols(x)]

        @pl.when(x == j)
        def _():
            pltpu.make_async_copy(grad_of.at[j, m], target, o_sem.at[m]).start()

        @pl.when(x != j)
        def _():
            send(grad_of.at[j, m], target, o_ss.at[j, m], o_sem.at[m], j, me)

    def backward_stage(step, carry):
        j = sections - 1 - step
        for m in ms:
            @pl.when(x == j)
            def _():
                expert_backward(j, m)

            relay(r_relay, r_recv, rr_sem, r_ss, r_sem, j, m)
        for m in ms:
            differ(j, m)
        for m in ms:
            pick_choice(j, m)

        @pl.when(x == j)
        def _():
            parameter_sums()

        for m in ms:
            backward_gather(j, m)

        @pl.when((x == j) & (lax.rem(me, stride) == 0))
        def _():
            owner_sum()

        for m in ms:
            backward_finish(j, m)
        return carry

    lax.fori_loop(0, sections, backward_stage, 0)

    wait_bytes(f_recv, f_sem)
    half = width // 2
    router_out[:, :half] = f_recv[:, 0, :].astype(F32) / denominator
    router_out[:, half:] = f_recv[:, 1, :].astype(F32) / denominator
    wait_bytes(t_recv, t_sem)
    for b in range(owners):
        gain_out[:, b * 128 : (b + 1) * 128] = t_recv[b]

    rest = pl.ds(0, experts - 1)
    for m in ms:
        wait_bytes(grad_of.at[pl.ds(0, sections), m], o_sem.at[m])
        wait_bytes(y_send.at[m, pl.ds(0, 3)], yr_ss.at[m])
        wait_bytes(r_send.at[m, pl.ds(0, 3)], rr_ss.at[m])
        wait_bytes(p_send.at[m, rest], p_ss.at[m])
    wait_bytes(gain_send.at[pl.ds(0, 3)], gain_ss)
    wait_bytes(give.at[pl.ds(0, 3)], give_ss)
    wait_bytes(router_send.at[pl.ds(0, 3)], router_ss)
    wait_bytes(f_recv.at[rest], f_ss)

    @pl.when(lax.rem(me, stride) == 0)
    def _():
        wait_bytes(s_send.at[pl.ds(0, owners - 1)], s_ss)
        wait_bytes(s_recv.at[rest], t_ss)

    @pl.when(lax.rem(me, stride) != 0)
    def _():
        wait_bytes(s_send, s_ss)

    def drain(j, carry):
        for m in ms:
            for buffer, sem in ((x_send, x_ss), (g_send, g_ss), (y_relay, y_ss), (r_relay, r_ss)):
                wait_bytes(buffer.at[j, m, rest], sem.at[j, m])
            for buffer, sem in ((norm_recv, norm_ss), (diff_recv, diff_ss), (inner_recv, inner_ss)):
                wait_bytes(buffer.at[j, m], sem.at[j, m])

            @pl.when(x != j)
            def _():
                wait_bytes(x_send.at[j, m, 0], x_ss.at[j, m])
                wait_bytes(g_send.at[j, m, 0], g_ss.at[j, m])
                wait_bytes(grad_of.at[j, m], o_ss.at[j, m])

        return carry

    lax.fori_loop(0, sections, drain, 0)


def solution(mesh):
    sections, experts = mesh.shape["section"], mesh.shape["expert"]

    def local(inputs, cotangent, lengths, norm_gain, router, expert_in, expert_out, routes):
        micros, tokens, width = inputs.shape
        hidden = expert_out.shape[2]
        piece = width // sections
        owners = width // 128
        slots = 2 * experts
        vmem = pl.BlockSpec(memory_space=pltpu.VMEM)
        hbm = pl.BlockSpec(memory_space=pl.ANY)
        DMA = pltpu.SemaphoreType.DMA
        steps = pltpu.VMEM((sections, micros, experts, 2, piece), BF16)
        parts = pltpu.VMEM((micros, sections, experts, 2, piece), BF16)
        small = pltpu.VMEM((micros, experts, 2, 128), BF16)
        stat = pltpu.VMEM((sections, micros, tokens, 128), F32)
        stats = pltpu.VMEM((sections, micros, sections - 1, tokens, 128), F32)
        rows = pltpu.VMEM((sections, 1, piece), F32)
        routing = pltpu.VMEM((sections, experts, piece), BF16)
        each, parted, single = DMA((sections, micros)), DMA((micros, sections)), DMA((micros,))
        grads, router_rows, gain_row = pl.pallas_call(
            functools.partial(kernel, experts, float(micros * 2 * tokens)),
            out_shape=(
                jax.ShapeDtypeStruct((1, micros, tokens, width), BF16),
                jax.ShapeDtypeStruct((experts, width), F32),
                jax.ShapeDtypeStruct((1, width), F32),
            ),
            in_specs=[hbm, hbm, vmem, vmem, vmem, hbm, hbm, vmem],
            out_specs=(hbm, vmem, vmem),
            scratch_shapes=[
                pltpu.VMEM((sections, piece, 2 * hidden), BF16),
                pltpu.VMEM((sections, hidden, piece), BF16),
                pltpu.VMEM((sections, micros, tokens, piece), BF16),
                pltpu.VMEM((sections + 1, micros, tokens, piece), BF16),
                pltpu.VMEM((sections, micros, 2 * tokens, slots), BF16),
                routing, routing, rows, rows,
                steps, parts, parts, steps, steps, steps, parts, parts, steps, steps,
                small, small,
                pltpu.VMEM((1, 2, width // 2), BF16),
                pltpu.VMEM((experts, 2, width // 2), BF16),
                pltpu.VMEM((owners, 1, 128), F32),
                pltpu.VMEM((experts, 1, 128), F32),
                pltpu.VMEM((1, 1, 128), F32),
                pltpu.VMEM((owners, 1, 128), F32),
                stat, stats, stat, stats, stat, stats, stat,
                pltpu.VMEM((micros, slots, 2 * hidden), F32),
                pltpu.VMEM((slots, 2 * hidden), BF16),
                pltpu.VMEM((micros, tokens, piece), F32),
                pltpu.VMEM((micros, slots, 128), F32),
                pltpu.VMEM((micros, tokens, experts), BF16),
                rows, rows,
                pltpu.SemaphoreType.REGULAR, DMA((2, sections)), single, single,
                DMA((sections,)), DMA((sections,)), DMA((sections,)),
                parted, each, each, parted, each, each, single, DMA, DMA, DMA,
                each, each, each, single,
                DMA, DMA, DMA, each, single, each, each, single, each, single, DMA, DMA, DMA,
                each, each, each, each,
            ],
            compiler_params=pltpu.CompilerParams(
                collective_id=0, has_side_effects=True, vmem_limit_bytes=60 * 1024 * 1024
            ),
        )(inputs, cotangent, lengths, norm_gain, router, expert_in, expert_out, routes)
        return grads, router_rows.T[None], gain_row

    in_specs = (
        P(None, "expert", None),
        P(None, "expert", None),
        P(None, "expert"),
        P("section", None),
        P("section", None, None),
        P("section", "expert", None, None),
        P("section", "expert", None, None),
        P("section", None, "expert", None),
    )
    out_specs = (P("section", None, "expert", None), P("section", None, None), P("section", None))
    return jax.shard_map(local, mesh=mesh, in_specs=in_specs, out_specs=out_specs, check_vma=False)
```

```python
import functools

import jax
import jax.numpy as jnp
from jax import lax
from jax.experimental import pallas as pl
from jax.experimental.pallas import tpu as pltpu
from jax.sharding import PartitionSpec as P

EPSILON = 1e-06
MESH = pl.DeviceIdType.MESH
F32 = jnp.float32
BF16 = jnp.bfloat16


def dot_nn(left, right):
    return jnp.dot(left, right, preferred_element_type=F32)


def dot_nt(left, right):
    return lax.dot_general(left, right, (((1,), (1,)), ((), ())), preferred_element_type=F32)


def dot_tn(left, right):
    return lax.dot_general(left, right, (((0,), (0,)), ((), ())), preferred_element_type=F32)


def wait_bytes(ref, sem):
    pltpu.make_async_copy(ref, ref, sem).wait()


def for_peers(me, experts, visit):
    if experts != 64:
        for step in range(1, experts):
            visit(lax.rem(me + step, experts))
        return
    my_z, my_y, my_core = me // 8, lax.rem(me // 2, 4), lax.rem(me, 2)
    near = [lax.rem(my_y + q // 2, 4) * 2 + lax.rem(my_core + q % 2, 2) for q in range(8)]

    def ring(step, carry):
        half = (step + 1) // 2
        base = lax.rem(my_z + 4 + half * (1 - 2 * lax.rem(step, 2)), 8) * 8
        for q in range(8):
            visit(base + near[q])
        return carry

    lax.fori_loop(0, 7, ring, 0)
    for q in range(1, 8):
        visit(my_z * 8 + near[q])


def for_half(me, experts, half, visit, own):
    if experts != 64:
        for peer in range(half * experts // 2, (half + 1) * experts // 2):
            pl.when(peer != me)(functools.partial(visit, peer))
            pl.when(peer == me)(own)
        return
    my_z, my_y, my_core = me // 8, lax.rem(me // 2, 4), lax.rem(me, 2)
    near = [lax.rem(my_y + q // 2, 4) * 2 + lax.rem(my_core + q % 2, 2) for q in range(8)]

    def ring(step, carry):
        z = half * 4 + lax.rem(my_z + 2 + step, 4)
        for q in range(1, 8):
            visit(z * 8 + near[q])
        pl.when(z != my_z)(lambda: visit(z * 8 + near[0]))
        pl.when(z == my_z)(own)
        return carry

    lax.fori_loop(0, 4, ring, 0)


def column_of(wide):
    return wide[:, :1]


def kernel(
    experts, denominator,
    inputs, cotangent, lengths, gain, router, w_in_hbm, w_out_hbm, routes,
    grads_out, router_out, gain_out,
    w_in, w_out, hidden_of, grad_of, give, router_send, router_of, gain_send, gain_of, gain_inverse,
    x_send, x_recv, y_send, y_relay, y_recv, g_send, g_recv, r_send, r_relay, r_recv,
    p_send, p_recv, f_send, f_recv, s_send, s_recv, t_send, t_recv,
    norm_send, norm_recv, diff_send, diff_recv, inner_send, inner_recv, norm_keep,
    mixed, joined, q_keep, row_scale, logit_keep, column, gain_part,
    plane_sem, weight_sem, h_sem, c_sem, give_sem, router_sem, gain_sem,
    x_sem, yr_sem, y_sem, g_sem, rr_sem, r_sem, p_sem, f_sem, s_sem, t_sem,
    norm_sem, diff_sem, inner_sem, o_sem,
    give_ss, router_ss, gain_ss, x_ss, yr_ss, y_ss, g_ss, rr_ss, r_ss, p_ss, f_ss, s_ss, t_ss,
    norm_ss, diff_ss, inner_ss, o_ss,
):
    x = lax.axis_index("section")
    me = lax.axis_index("expert")
    micros, tokens, width = inputs.shape
    sections = 4
    hidden = w_out.shape[1]
    slots = 2 * experts
    piece = width // sections
    owners = s_send.shape[0]
    stride = experts // owners
    ms = range(micros)

    def cols(q):
        return pl.ds(pl.multiple_of(q * piece, piece), piece)

    def send(source, target, send_sem, recv_sem, section, expert):
        pltpu.make_async_remote_copy(
            src_ref=source, dst_ref=target, send_sem=send_sem, recv_sem=recv_sem,
            device_id={"section": section, "expert": expert}, device_id_type=MESH,
        ).start()

    for m in ms:
        pltpu.make_async_copy(inputs.at[m, :, cols(x)], hidden_of.at[0, m], h_sem.at[m]).start()
    loads = []
    for q in range(sections):
        loads.append(pltpu.make_async_copy(w_in_hbm.at[0, 0, pl.ds(q * piece, piece)], w_in.at[q], weight_sem.at[0, q]))
    for q in range(sections):
        loads.append(pltpu.make_async_copy(w_out_hbm.at[0, 0, :, pl.ds(q * piece, piece)], w_out.at[q], weight_sem.at[1, q]))
    for load in loads:
        load.start()
    for m in ms:
        pltpu.make_async_copy(cotangent.at[m, :, cols(x)], grad_of.at[sections, m], c_sem.at[m]).start()

    barrier = pltpu.get_barrier_semaphore()

    def greet(peer):
        pl.semaphore_signal(barrier, inc=1, device_id={"section": x, "expert": peer}, device_id_type=MESH)

    for_peers(me, experts, greet)
    others = [lax.rem(x + step, sections) for step in (1, 3, 2)]
    for other in others:
        pl.semaphore_signal(barrier, inc=1, device_id={"section": other, "expert": me}, device_id_type=MESH)

    column[...] = jnp.zeros_like(column)
    gain_part[...] = jnp.zeros_like(gain_part)
    expert_codes = lax.broadcasted_iota(jnp.int32, (tokens, experts), 1)
    earlier = (
        lax.broadcasted_iota(jnp.int32, (tokens, tokens), 1)
        < lax.broadcasted_iota(jnp.int32, (tokens, tokens), 0)
    ).astype(F32).astype(BF16)
    slot_codes = lax.broadcasted_iota(jnp.int32, (tokens, slots), 1).astype(F32)
    positions = lax.broadcasted_iota(jnp.int32, (tokens, 1), 0)
    for m in ms:
        live = positions < lengths[m : m + 1, :]
        tables = []
        for k in range(2):
            choice = routes[0, m][:, k : k + 1]
            marked = (choice == expert_codes).astype(F32)
            rank = jnp.sum(marked * dot_nn(earlier, marked.astype(BF16)), axis=1, keepdims=True)
            slot = choice.astype(F32) * 2.0 + rank
            tables.append(((slot == slot_codes) & live).astype(F32))
        give[x, m] = jnp.concatenate(tables, axis=0).astype(BF16)
    eye = (
        lax.broadcasted_iota(jnp.int32, (experts, experts), 0)
        == lax.broadcasted_iota(jnp.int32, (experts, experts), 1)
    ).astype(F32).astype(BF16)
    for q in range(sections):
        router_send[q] = dot_nt(eye, router[0, q * piece : (q + 1) * piece, :]).astype(BF16)
        gain_send[q] = gain[:, q * piece : (q + 1) * piece]
        gain_inverse[q] = 1.0 / gain_send[q]
    router_of[x] = router_send[x]
    gain_of[x] = gain_send[x]
    fold = (
        lax.broadcasted_iota(jnp.int32, (slots, experts), 0) // 2
        == lax.broadcasted_iota(jnp.int32, (slots, experts), 1)
    ).astype(F32).astype(BF16)

    pl.semaphore_wait(barrier, experts - 1 + sections - 1)
    for other in others:
        pl.semaphore_signal(plane_sem, inc=1, device_id={"section": other, "expert": me}, device_id_type=MESH)

    def publish():
        for other in others:
            send(gain_send.at[other], gain_of.at[x], gain_ss, gain_sem.at[x], other, me)
            send(give.at[x], give.at[x], give_ss, give_sem.at[x], other, me)
        for other in others:
            send(router_send.at[other], router_of.at[x], router_ss, router_sem.at[x], other, me)

    pl.when(x == 0)(publish)
    pl.semaphore_wait(plane_sem, sections - 1)

    def share(values, sends, receives, send_sem, recv_sem, j, m):
        sends[j, m] = jnp.concatenate([values] * (128 // tokens), axis=0).T[:8]
        for slot, other in enumerate(others):
            send(sends.at[j, m], receives.at[j, m, slot], send_sem.at[j, m], recv_sem.at[j, m], other, me)

    def shared(sends, receives, recv_sem, j, m):
        wait_bytes(receives.at[j, m], recv_sem.at[j, m])
        total = sends[j, m] + receives[j, m, 0] + receives[j, m, 1] + receives[j, m, 2]
        return jnp.concatenate([total] * 16, axis=0).T[:tokens]

    def wide(values):
        return jnp.broadcast_to(values, (tokens, 128))

    def signs(j, m):
        return dot_nn(give[j, m, :tokens] - give[j, m, tokens:], fold)

    def scales(j, m):
        total = norm_keep[j, m]
        scale = lax.rsqrt(total[:, 0:1] / width + EPSILON)
        margin = total[:, 1:2] * scale
        return scale, jax.nn.sigmoid(margin), jax.nn.sigmoid(-margin)

    def dispatch(values, sends, receives, send_sem, recv_sem, j, m):
        sends[j, m] = dot_tn(give[j, m], values).astype(BF16).reshape(experts, 2, piece)
        target, arrive, leave = receives.at[m, x, me], recv_sem.at[m, x], send_sem.at[j, m]
        for_peers(me, experts, lambda peer: send(sends.at[j, m, peer], target, leave, arrive, j, peer))

        @pl.when(x == j)
        def _():
            pltpu.make_async_copy(sends.at[j, m, me], target, arrive).start()

        @pl.when(x != j)
        def _():
            send(sends.at[j, m, me], target, leave, arrive, j, me)

    def forward_send(j, m):
        values = hidden_of[j, m].astype(F32)
        rows = (values * gain_of[j]).astype(BF16)
        dispatch(jnp.concatenate([rows, rows], axis=0), x_send, x_recv, x_ss, x_sem, j, m)
        if m == 0:
            @pl.when(x != j)
            def _():
                wait_bytes(router_of.at[j], router_sem.at[j])

        logits = dot_nt(rows, router_of[j])
        margin = jnp.sum(signs(j, m) * logits, axis=1, keepdims=True)
        square = jnp.sum(values * values, axis=1, keepdims=True)
        lanes = lax.broadcasted_iota(jnp.int32, (tokens, 128), 1)
        share(jnp.where(lanes == 0, square, jnp.where(lanes == 1, margin, 0.0)), norm_send, norm_recv, norm_ss, norm_sem, j, m)

    def settle(j, m):
        norm_keep[j, m] = shared(norm_send, norm_recv, norm_sem, j, m)

    def backward_send(j, m):
        _, first, second = scales(j, m)
        grad = grad_of[j + 1, m].astype(F32)
        pair = jnp.concatenate([(first * grad).astype(BF16), (second * grad).astype(BF16)], axis=0)
        dispatch(pair, g_send, g_recv, g_ss, g_sem, j, m)

    def bulk(sends, receives, send_sem, recv_sem, j, m, q):
        for half in range(2):
            part = pl.ds(half * experts // 2, experts // 2)
            send(sends.at[m, q, part], receives.at[j, m, part], send_sem.at[m], recv_sem.at[j, m, half], q, me)

    near_first = [lax.rem(x + step, sections) for step in (0, 1, 3, 2)]
    far_first = [lax.rem(x + step, sections) for step in (2, 1, 3)]

    def expert_forward(j, m):
        square = jnp.zeros((slots, 1), F32)
        for index, q in enumerate(near_first):
            wait_bytes(x_recv.at[m, q], x_sem.at[m, q])
            rows = x_recv[m, q].reshape(slots, piece)
            if m == 0:
                wait_bytes(w_in.at[q], weight_sem.at[0, q])
            part = dot_nn(rows, w_in[q])
            mixed[m] = part if index == 0 else mixed[m] + part
            plain = rows.astype(F32) * gain_inverse[q]
            square += jnp.sum(plain * plain, axis=1, keepdims=True)
        scale = lax.rsqrt(square / width + EPSILON)
        row_scale[m] = jnp.broadcast_to(scale, (slots, 128))
        gate, up = mixed[m, :, :hidden] * scale, mixed[m, :, hidden:] * scale
        mixed[m, :, :hidden] = gate
        mixed[m, :, hidden:] = up
        activated = (gate * jax.nn.sigmoid(gate) * up).astype(BF16)
        for q in far_first + [x]:
            if m == 0:
                wait_bytes(w_out.at[q], weight_sem.at[1, q])
            result = dot_nn(activated, w_out[q]).astype(BF16).reshape(experts, 2, piece)
            if q is x:
                y_relay[j, m] = result
            else:
                y_send[m, q] = result
                bulk(y_send, y_relay, yr_ss, yr_sem, j, m, q)

    def relay(buffer, target, bulk_sem, send_sem, recv_sem, j, m):
        own = target.at[j, m, me]
        for half in range(2):
            @pl.when(x != j)
            def _():
                wait_bytes(buffer.at[j, m, pl.ds(half * experts // 2, experts // 2)], bulk_sem.at[j, m, half])

            for_half(
                me, experts, half,
                lambda peer: send(buffer.at[j, m, peer], own, send_sem.at[j, m], recv_sem.at[j, m], x, peer),
                lambda: pltpu.make_async_copy(buffer.at[j, m, me], own, recv_sem.at[j, m]).start(),
            )

    def choices(j, m):
        return dot_nn(give[j, m], y_recv[j, m].reshape(slots, piece))

    def forward_combine(j, m):
        wait_bytes(y_recv.at[j, m], y_sem.at[j, m])
        per_choice = choices(j, m)
        _, first, second = scales(j, m)
        combined = first * per_choice[:tokens] + second * per_choice[tokens:]
        hidden_of[j + 1, m] = (hidden_of[j, m].astype(F32) + combined).astype(BF16)

    def learn(j):
        @pl.when(x != j)
        def _():
            wait_bytes(gain_of.at[j], gain_sem.at[j])
            wait_bytes(give.at[j], give_sem.at[j])

    learn(0)
    for m in ms:
        wait_bytes(hidden_of.at[0, m], h_sem.at[m])
        forward_send(0, m)
    pl.when(x != 0)(publish)
    for m in ms:
        settle(0, m)

    def forward_stage(j, carry):
        for m in ms:
            @pl.when(x == j)
            def _():
                expert_forward(j, m)

            relay(y_relay, y_recv, yr_sem, y_ss, y_sem, j, m)

        @pl.when(j < sections - 1)
        def _():
            learn(j + 1)
            for m in ms:
                forward_combine(j, m)
                forward_send(j + 1, m)
            for m in ms:
                settle(j + 1, m)

        @pl.when(j == sections - 2)
        def _():
            for m in ms:
                wait_bytes(grad_of.at[sections, m], c_sem.at[m])
                backward_send(sections - 1, m)

        return carry

    lax.fori_loop(0, sections, forward_stage, 0)

    def expert_backward(j, m):
        for index, q in enumerate(near_first):
            wait_bytes(g_recv.at[m, q], g_sem.at[m, q])
            part = dot_nt(g_recv[m, q].reshape(slots, piece), w_out[q])
            act_grad = part if index == 0 else act_grad + part
        gate, up = mixed[m, :, :hidden], mixed[m, :, hidden:]
        sigmoid_gate = jax.nn.sigmoid(gate)
        joined[:, :hidden] = (act_grad * up * sigmoid_gate * (1.0 + gate * (1.0 - sigmoid_gate))).astype(BF16)
        joined[:, hidden:] = (act_grad * gate * sigmoid_gate).astype(BF16)
        for q in far_first + [x]:
            result = dot_nt(joined[...], w_in[q]).astype(BF16).reshape(experts, 2, piece)
            r_send[m, q] = result
            if q is x:
                r_relay[j, m] = result
            else:
                bulk(r_send, r_relay, rr_ss, rr_sem, j, m, q)

    def differ(j, m):
        @pl.when(j == sections - 1)
        def _():
            wait_bytes(y_recv.at[j, m], y_sem.at[j, m])

        per_choice = choices(j, m)
        grad = grad_of[j + 1, m].astype(F32)
        difference = jnp.sum(grad * (per_choice[:tokens] - per_choice[tokens:]), axis=1, keepdims=True)
        share(wide(difference), diff_send, diff_recv, diff_ss, diff_sem, j, m)

    def pick_choice(j, m):
        difference = column_of(shared(diff_send, diff_recv, diff_sem, j, m))
        _, first, second = scales(j, m)
        pick = first * second * difference
        logit_keep[m] = (pick * signs(j, m)).astype(BF16)

        @pl.when(x == j)
        def _():
            lanes = lax.broadcasted_iota(jnp.int32, (2 * tokens, 128), 1)
            picks = jnp.where(lanes == 0, jnp.concatenate([pick, -pick], axis=0), 0.0).astype(BF16)
            p_send[m] = dot_tn(give[j, m], picks).astype(BF16).reshape(experts, 2, 128)
            own = p_recv.at[m, me]
            pltpu.make_async_copy(p_send.at[m, me], own, p_sem.at[m]).start()
            for_peers(me, experts, lambda peer: send(p_send.at[m, peer], own, p_ss.at[m], p_sem.at[m], x, peer))

    def parameter_sums():
        for m in ms:
            wait_bytes(p_recv.at[m], p_sem.at[m])
            scale = column_of(row_scale[m])
            weight = p_recv[m].reshape(slots, 128)[:, :1].astype(F32) * scale
            for q in range(sections):
                rows = x_recv[m, q].reshape(slots, piece).astype(F32)
                row_grads = r_send[m, q].reshape(slots, piece).astype(F32)
                column[q] += jnp.sum(rows * weight, axis=0, keepdims=True)
                gain_part[q] += jnp.sum(row_grads * (rows * scale), axis=0, keepdims=True)
        mine = (lax.broadcasted_iota(jnp.int32, (8, experts), 1) == me).astype(F32).astype(BF16)
        for q in range(sections):
            own_router = dot_nn(mine, router_send[q])[:1]
            total = (gain_part[q] + own_router * column[q]) / gain_send[q]
            for b in range(owners // sections):
                s_send[q * (owners // sections) + b] = total[:, b * 128 : (b + 1) * 128]
        f_send[0] = jnp.concatenate(
            [jnp.concatenate([column[0], column[1]], axis=1), jnp.concatenate([column[2], column[3]], axis=1)], axis=0
        ).astype(BF16)
        for b in range(owners):
            @pl.when(me == b * stride)
            def _():
                pltpu.make_async_copy(s_send.at[b], s_recv.at[me], s_sem).start()

            @pl.when(me != b * stride)
            def _():
                send(s_send.at[b], s_recv.at[me], s_ss, s_sem, x, b * stride)

        pltpu.make_async_copy(f_send.at[0], f_recv.at[me], f_sem).start()
        for_peers(me, experts, lambda peer: send(f_send.at[0], f_recv.at[me], f_ss, f_sem, x, peer))

    def owner_sum():
        wait_bytes(s_recv, s_sem)
        t_send[0] = jnp.sum(s_recv[:, 0, :], axis=0, keepdims=True) / denominator
        own = t_recv.at[me // stride]
        pltpu.make_async_copy(t_send.at[0], own, t_sem).start()
        for_peers(me, experts, lambda peer: send(t_send.at[0], own, t_ss, t_sem, x, peer))

    def backward_gather(j, m):
        wait_bytes(r_recv.at[j, m], r_sem.at[j, m])
        both = give[j, m, :tokens] + give[j, m, tokens:]
        scaled = (
            dot_nn(both, r_recv[j, m].reshape(slots, piece)) + dot_nn(logit_keep[m], router_of[j])
        ) * gain_of[j]
        q_keep[m] = scaled
        scale, _, _ = scales(j, m)
        inner = jnp.sum(scaled * (hidden_of[j, m].astype(F32) * scale), axis=1, keepdims=True)
        share(wide(inner), inner_send, inner_recv, inner_ss, inner_sem, j, m)

    def backward_finish(j, m):
        scale, _, _ = scales(j, m)
        inner = column_of(shared(inner_send, inner_recv, inner_sem, j, m)) / width
        centred = hidden_of[j, m].astype(F32) * scale
        grad = grad_of[j + 1, m].astype(F32)
        grad_of[j, m] = (grad + scale * (q_keep[m] - centred * inner)).astype(BF16)

        @pl.when(j > 0)
        def _():
            backward_send(j - 1, m)

        target = grads_out.at[0, m, :, cols(x)]

        @pl.when(x == j)
        def _():
            pltpu.make_async_copy(grad_of.at[j, m], target, o_sem.at[m]).start()

        @pl.when(x != j)
        def _():
            send(grad_of.at[j, m], target, o_ss.at[j, m], o_sem.at[m], j, me)

    def pick_all(j):
        for m in ms:
            differ(j, m)
        for m in ms:
            pick_choice(j, m)

    def backward_stage(step, carry):
        j = sections - 1 - step
        for m in ms:
            @pl.when(x == j)
            def _():
                expert_backward(j, m)

            relay(r_relay, r_recv, rr_sem, r_ss, r_sem, j, m)

        @pl.when(j == sections - 1)
        def _():
            pick_all(j)

        @pl.when((j == 0) & (x == 0))
        def _():
            parameter_sums()

        for m in ms:
            backward_gather(j, m)
            backward_finish(j, m)
            if m == 0:
                @pl.when((j == 0) & (lax.rem(me, stride) == 0))
                def _():
                    owner_sum()

        @pl.when(j > 0)
        def _():
            pick_all(j - 1)

            @pl.when(x == j)
            def _():
                parameter_sums()

        return carry

    lax.fori_loop(0, sections, backward_stage, 0)

    wait_bytes(f_recv, f_sem)
    half = width // 2
    router_out[:, :half] = f_recv[:, 0, :].astype(F32) / denominator
    router_out[:, half:] = f_recv[:, 1, :].astype(F32) / denominator
    wait_bytes(t_recv, t_sem)
    for b in range(owners):
        gain_out[:, b * 128 : (b + 1) * 128] = t_recv[b]

    rest = pl.ds(0, experts - 1)
    for m in ms:
        wait_bytes(grad_of.at[pl.ds(0, sections), m], o_sem.at[m])
        wait_bytes(y_send.at[m, pl.ds(0, 3)], yr_ss.at[m])
        wait_bytes(r_send.at[m, pl.ds(0, 3)], rr_ss.at[m])
        wait_bytes(p_send.at[m, rest], p_ss.at[m])
    wait_bytes(gain_send.at[pl.ds(0, 3)], gain_ss)
    wait_bytes(give.at[pl.ds(0, 3)], give_ss)
    wait_bytes(router_send.at[pl.ds(0, 3)], router_ss)
    wait_bytes(f_recv.at[rest], f_ss)

    @pl.when(lax.rem(me, stride) == 0)
    def _():
        wait_bytes(s_send.at[pl.ds(0, owners - 1)], s_ss)
        wait_bytes(s_recv.at[rest], t_ss)

    @pl.when(lax.rem(me, stride) != 0)
    def _():
        wait_bytes(s_send, s_ss)

    def drain(j, carry):
        for m in ms:
            for buffer, sem in ((x_send, x_ss), (g_send, g_ss), (y_relay, y_ss), (r_relay, r_ss)):
                wait_bytes(buffer.at[j, m, rest], sem.at[j, m])
            for buffer, sem in ((norm_recv, norm_ss), (diff_recv, diff_ss), (inner_recv, inner_ss)):
                wait_bytes(buffer.at[j, m], sem.at[j, m])

            @pl.when(x != j)
            def _():
                wait_bytes(x_send.at[j, m, 0], x_ss.at[j, m])
                wait_bytes(g_send.at[j, m, 0], g_ss.at[j, m])
                wait_bytes(grad_of.at[j, m], o_ss.at[j, m])

        return carry

    lax.fori_loop(0, sections, drain, 0)


def solution(mesh):
    sections, experts = mesh.shape["section"], mesh.shape["expert"]

    def local(inputs, cotangent, lengths, norm_gain, router, expert_in, expert_out, routes):
        micros, tokens, width = inputs.shape
        hidden = expert_out.shape[2]
        piece = width // sections
        owners = width // 128
        slots = 2 * experts
        vmem = pl.BlockSpec(memory_space=pltpu.VMEM)
        hbm = pl.BlockSpec(memory_space=pl.ANY)
        DMA = pltpu.SemaphoreType.DMA
        steps = pltpu.VMEM((sections, micros, experts, 2, piece), BF16)
        parts = pltpu.VMEM((micros, sections, experts, 2, piece), BF16)
        small = pltpu.VMEM((micros, experts, 2, 128), BF16)
        stat = pltpu.VMEM((sections, micros, 8, 128), F32)
        stats = pltpu.VMEM((sections, micros, sections - 1, 8, 128), F32)
        kept = pltpu.VMEM((sections, micros, tokens, 128), F32)
        rows = pltpu.VMEM((sections, 1, piece), F32)
        routing = pltpu.VMEM((sections, experts, piece), BF16)
        halved = DMA((sections, micros, 2))
        each, parted, single = DMA((sections, micros)), DMA((micros, sections)), DMA((micros,))
        grads, router_rows, gain_row = pl.pallas_call(
            functools.partial(kernel, experts, float(micros * 2 * tokens)),
            out_shape=(
                jax.ShapeDtypeStruct((1, micros, tokens, width), BF16),
                jax.ShapeDtypeStruct((experts, width), F32),
                jax.ShapeDtypeStruct((1, width), F32),
            ),
            in_specs=[hbm, hbm, vmem, vmem, vmem, hbm, hbm, vmem],
            out_specs=(hbm, vmem, vmem),
            scratch_shapes=[
                pltpu.VMEM((sections, piece, 2 * hidden), BF16),
                pltpu.VMEM((sections, hidden, piece), BF16),
                pltpu.VMEM((sections, micros, tokens, piece), BF16),
                pltpu.VMEM((sections + 1, micros, tokens, piece), BF16),
                pltpu.VMEM((sections, micros, 2 * tokens, slots), BF16),
                routing, routing, rows, rows, rows,
                steps, parts, parts, steps, steps, steps, parts, parts, steps, steps,
                small, small,
                pltpu.VMEM((1, 2, width // 2), BF16),
                pltpu.VMEM((experts, 2, width // 2), BF16),
                pltpu.VMEM((owners, 1, 128), F32),
                pltpu.VMEM((experts, 1, 128), F32),
                pltpu.VMEM((1, 1, 128), F32),
                pltpu.VMEM((owners, 1, 128), F32),
                stat, stats, stat, stats, stat, stats, kept,
                pltpu.VMEM((micros, slots, 2 * hidden), F32),
                pltpu.VMEM((slots, 2 * hidden), BF16),
                pltpu.VMEM((micros, tokens, piece), F32),
                pltpu.VMEM((micros, slots, 128), F32),
                pltpu.VMEM((micros, tokens, experts), BF16),
                rows, rows,
                pltpu.SemaphoreType.REGULAR, DMA((2, sections)), single, single,
                DMA((sections,)), DMA((sections,)), DMA((sections,)),
                parted, halved, each, parted, halved, each, single, DMA, DMA, DMA,
                each, each, each, single,
                DMA, DMA, DMA, each, single, each, each, single, each, single, DMA, DMA, DMA,
                each, each, each, each,
            ],
            compiler_params=pltpu.CompilerParams(
                collective_id=0, has_side_effects=True, vmem_limit_bytes=60 * 1024 * 1024
            ),
        )(inputs, cotangent, lengths, norm_gain, router, expert_in, expert_out, routes)
        return grads, router_rows.T[None], gain_row

    in_specs = (
        P(None, "expert", None),
        P(None, "expert", None),
        P(None, "expert"),
        P("section", None),
        P("section", None, None),
        P("section", "expert", None, None),
        P("section", "expert", None, None),
        P("section", None, "expert", None),
    )
    out_specs = (P("section", None, "expert", None), P("section", None, None), P("section", None))
    return jax.shard_map(local, mesh=mesh, in_specs=in_specs, out_specs=out_specs, check_vma=False)
```
